32 devices in a mesh: layer: 2 (over y), row: 4 (over z), col: 4 (over x, core).
Axes of the slice: x: 2, y: 2, z: 4, core: 2. Of those that a mesh axis runs over, the one named last changes fastest.
Arguments:
- leaf_sol: bfloat16 [8, 256, 256], P(('layer', 'col'), 'row'), may hold values from -6 to 6
- lower_blocks: bfloat16 [8192, 1024], P(('layer', 'row'), 'col'), may hold values from -0.1875 to 0.1875
- lower_mask: int32 [32, 4], P(('layer', 'row'), 'col'), may hold values 0 or 1
- upper_blocks: bfloat16 [2048, 4096], P(('layer', 'col'), 'row'), may hold values from -0.125 to 0.125
- upper_mask: int32 [8, 16], P(('layer', 'col'), 'row'), may hold values 0 or 1
- anc_rhs: bfloat16 [4096, 256], P(('row', 'col')), may hold values from -6 to 6
- diag_inv: bfloat16 [4096, 256], P(('row', 'col')), may hold values from -0.375 to 0.375
Outputs:
- new_leaves: bfloat16 [8, 256, 256], P(('layer', 'col'), 'row')
- anc_sol: bfloat16 [4096, 256], P(('row', 'col'))
The draws below stay inside these ranges and needn't reach their ends.
Inputs may be any that keep to these rules, and one draw needn't show every extreme that they name: `lower_mask`: 1 marks a stored block of L. `upper_mask`: 1 marks a stored block of U.
All inputs are finite; a program needn't handle non-finite values.
Results may differ from the reference program's by a relative error of at most 0.0044.
Values may be sent and summed in bfloat16 or wider, within the bound.
A program may use at most 64 MiB of HBM per device.

```python
import jax
import jax.numpy as jnp
from jax import lax

BS = 256
RHS = 256
ANC = 4096
LEAF = 1024
N_LAYER = 2
N_COL = 4


def plant(drawn, stream_key, low, largest):
    longest = drawn.shape.index(max(drawn.shape))
    spots = []
    for shift in (0, 1):
        where = [jax.random.randint(jax.random.fold_in(stream_key, axis), (), 0, length) for axis, length in enumerate(drawn.shape)]
        where[longest] = (where[longest] + shift) % drawn.shape[longest]
        spots.append(tuple(where))
    return drawn.at[spots[0]].set(low).at[spots[1]].set(largest)


def steps_of(stream_key, dims, pieces, smallest, top_value):
    def one(position, blocks):
        steps = jax.random.uniform(jax.random.fold_in(jax.random.fold_in(stream_key, 6), position), (blocks,), jnp.float32, smallest / len(pieces), top_value / len(pieces))
        return jnp.repeat(jnp.exp(steps), dims[position] // blocks).reshape((-1,) + (1,) * (len(dims) - position - 1))

    level = one(*pieces[0])
    for cut in pieces[1:]:
        level = level * one(*cut)
    return level


def gaussian(own_key, dims, width, limit, pieces=(), kind=jnp.bfloat16):
    factor_of = steps_of(own_key, dims, pieces, -0.22, 0.18) if pieces else 1.0
    entries = jax.random.normal(own_key, dims, jnp.float32) * width * factor_of
    return jnp.minimum(jnp.maximum(entries, -limit), limit).astype(kind)


def setup_inputs(seed: int = 0) -> dict:
    arg_keys = jax.random.split(jax.random.key(seed), 8)
    return {
        "leaf_sol": gaussian(arg_keys[0], (N_LAYER * N_COL, LEAF // N_COL, RHS), 1.0, 6.0, ((0, 8), (1, 4))),
        "lower_blocks": gaussian(arg_keys[1], (N_LAYER * ANC, LEAF), (LEAF * N_LAYER // 2) ** -0.5, 0.1875, ((0, 8), (1, 4))),
        "lower_mask": plant((jax.random.randint(arg_keys[2], (N_LAYER * ANC // BS, LEAF // BS), 0, 2) < 1).astype(jnp.int32), jax.random.fold_in(arg_keys[2], 1), 0, 1),
        "upper_blocks": gaussian(arg_keys[3], (N_LAYER * LEAF, ANC), (ANC // 2) ** -0.5, 0.125, ((0, 8), (1, 4))),
        "upper_mask": plant((jax.random.randint(arg_keys[4], (N_LAYER * LEAF // BS, ANC // BS), 0, 2) < 1).astype(jnp.int32), jax.random.fold_in(arg_keys[4], 1), 0, 1),
        "anc_rhs": gaussian(arg_keys[5], (ANC, RHS), 1.0, 6.0, ((0, 16),)),
        "diag_inv": gaussian(arg_keys[6], (ANC, BS), BS ** -0.5, 0.375, ((0, 16),)),
    }


def expand(mask, block):
    first, second = mask.shape
    full = jnp.broadcast_to(mask[:, None, :, None], (first, block, second, block))
    return full.reshape(first * block, second * block)


def reference(leaf_sol, lower_blocks, lower_mask, upper_blocks, upper_mask, anc_rhs, diag_inv):
    anc_blocks = ANC // BS
    leaf_count = LEAF // BS
    leaf_all = leaf_sol.reshape(N_LAYER, LEAF, RHS)

    def lower_layer(layer_id):
        band = lax.dynamic_slice_in_dim(lower_blocks, layer_id * ANC, ANC, 0)
        marks = lax.dynamic_slice_in_dim(lower_mask, layer_id * anc_blocks, anc_blocks, 0)
        masked = band * expand(marks, BS).astype(jnp.bfloat16)
        solved = lax.dynamic_index_in_dim(leaf_all, layer_id, 0, keepdims=False)
        return jnp.dot(masked, solved, preferred_element_type=jnp.float32)

    layers = jnp.arange(N_LAYER, dtype=jnp.int32)
    summed = jnp.sum(lax.map(lower_layer, layers), axis=0)
    remain = anc_rhs.astype(jnp.float32) - summed
    inverse = diag_inv.reshape(anc_blocks, BS, BS).astype(jnp.float32)
    solved_anc = jnp.einsum("kij,kjr->kir", inverse, remain.reshape(anc_blocks, BS, RHS),
                            precision=lax.Precision.HIGHEST)
    anc_sol = solved_anc.reshape(ANC, RHS).astype(jnp.bfloat16)

    def upper_layer(layer_id):
        band = lax.dynamic_slice_in_dim(upper_blocks, layer_id * LEAF, LEAF, 0)
        marks = lax.dynamic_slice_in_dim(upper_mask, layer_id * leaf_count, leaf_count, 0)
        masked = band * expand(marks, BS).astype(jnp.bfloat16)
        correct = jnp.dot(masked, anc_sol, preferred_element_type=jnp.float32)
        solved = lax.dynamic_index_in_dim(leaf_all, layer_id, 0, keepdims=False)
        return (solved.astype(jnp.float32) - correct).astype(jnp.bfloat16)

    new_leaves = lax.map(upper_layer, layers).reshape(leaf_sol.shape)
    return new_leaves, anc_sol
```

```python
import contextlib
import functools

import jax
import jax.numpy as jnp
from jax import lax
from jax.experimental import pallas as pl
from jax.experimental.pallas import tpu as pltpu
from jax.sharding import PartitionSpec as P

MESH = pl.DeviceIdType.MESH
scope = lambda name: contextlib.nullcontext()


def dot_last(a, b):
    return lax.dot_general(a, b, (((1,), (1,)), ((), ())), preferred_element_type=jnp.float32)


def await_bytes(ref, sem):
    pltpu.make_async_copy(ref, ref, sem).wait()


def kernel(
    n_layer, n_row, n_col, chunks,
    leaf, lower, lower_marks, upper, upper_marks, rhs, inv,
    new_leaves, anc_out,
    lower_mask, upper_mask, leaf_v, lower_all, upper_all, rhs_all, inv_all, x_all, rhs_t,
    held, part, part_in, anc_t, anc_other, fold, fold_in,
    local_sem, pair_send, pair_recv, x_send, x_recv, part_send, part_recv,
    anc_send, anc_recv, fold_send, fold_recv, near,
):
    layer = lax.axis_index("layer")
    row = lax.axis_index("row")
    col = lax.axis_index("col")
    halves = n_col // 2
    shares = n_layer // 2
    half, side = col // 2, lax.rem(col, 2)
    other = 1 - side
    partner = half * 2 + other
    parity, quota = lax.rem(layer, 2), layer // 2
    block = inv.shape[0]
    strip, width = leaf_v.shape
    wide = width // 2
    span = wide // chunks
    share = span // shares
    depth = n_row * strip
    group = [
        (dh, dp, dq) for dh in reversed(range(halves)) for dp in reversed(range(2)) for dq in reversed(range(shares))
    ][:-1]

    def number(dh, dp, dq):
        return (dh * 2 + dp) * shares + dq - 1

    def back(dh, dp, dq):
        return (halves - dh) % halves, dp, (shares - dq) % shares

    def peer(dh, dp, dq):
        to_layer = lax.rem(quota + dq, shares) * 2 + lax.rem(layer + dp, 2)
        return to_layer, row, lax.rem(half + dh, halves) * 2 + side

    def straight(dh, dp, dq):
        return dh == 0 or (dp, dq) == (0, 0)

    barrier = pltpu.get_barrier_semaphore()

    def greet(*device):
        pl.semaphore_signal(barrier, inc=1, device_id=device, device_id_type=MESH)

    for dr in reversed(range(1, n_row)):
        greet(layer, lax.rem(row + dr, n_row), col)
        greet(layer, lax.rem(row + dr, n_row), partner)
    greet(layer, row, partner)
    straights = [step for step in group if straight(*step)]
    for step in straights:
        greet(*peer(*step))

    def columns(which):
        return pl.ds(pl.multiple_of(which * wide, wide), wide)

    loads = [
        pltpu.make_async_copy(source, target, local_sem.at[index])
        for index, (source, target) in enumerate(
            (
                (lower_marks, lower_mask), (lower, lower_all.at[0]), (upper_marks, upper_mask), (upper, upper_all.at[0]),
                (rhs.at[:, columns(side)], rhs_all.at[0]), (inv, inv_all.at[0]), (leaf.at[0], leaf_v),
                (leaf.at[0, :, columns(side)], x_all.at[side * n_row + row]),
            )
        )
    ]
    for load in loads:
        load.start()
    with scope("A_bar"):
        pl.semaphore_wait(barrier, 2 * (n_row - 1) + 1 + len(straights))

    def x_copy(dr, to_side):
        return pltpu.make_async_remote_copy(
            src_ref=leaf.at[0, :, columns(to_side)], dst_ref=x_all.at[side * n_row + row],
            send_sem=x_send.at[0], recv_sem=x_recv.at[0],
            device_id=(layer, lax.rem(row + dr, n_row), half * 2 + to_side), device_id_type=MESH,
        )

    for dr in reversed(range(n_row)):
        for to_side in (side, other) if dr else (other,):
            x_copy(dr, to_side).start()

    def pair_copy(index, source, target):
        return pltpu.make_async_remote_copy(
            src_ref=source, dst_ref=target, send_sem=pair_send.at[index], recv_sem=pair_recv.at[index],
            device_id=(layer, row, partner), device_id_type=MESH,
        )

    lower_pair = pair_copy(0, lower_all.at[0], lower_all.at[1])
    upper_pair = pair_copy(1, upper_all.at[0], upper_all.at[1])
    rhs_pair = pair_copy(2, rhs.at[:, columns(other)], rhs_all.at[1])
    inv_pair = pair_copy(3, inv, inv_all.at[1])
    rhs_pair.start()
    inv_pair.start()
    for step in straights:
        if step[0] == 0:
            pl.semaphore_signal(near, inc=1, device_id=peer(*step), device_id_type=MESH)

    def apply_marks(blocks, marks, transposed):
        for down in range(blocks.shape[1] // block):
            for across in range(blocks.shape[2] // block):
                place = 0, slice(down * block, (down + 1) * block), slice(across * block, (across + 1) * block)
                mark = marks[across, down] if transposed else marks[down, across]
                blocks[place] = blocks[place] * jnp.full((block, block), mark.astype(jnp.float32)).astype(jnp.bfloat16)

    with scope("B_lower"):
        loads[0].wait()
        loads[1].wait()
        apply_marks(lower_all, lower_mask, True)
        lower_pair.start()
    with scope("C_upper"):
        loads[2].wait()
        loads[3].wait()
        apply_marks(upper_all, upper_mask, False)
        upper_pair.start()
    with scope("D_rhs"):
        loads[4].wait()
        loads[5].wait()
        loads[6].wait()
        rhs_pair.wait_recv()
        inv_pair.wait_recv()
        chosen = lax.rem(layer + side, 2)
        rhs_t[...] = rhs_all[chosen].astype(jnp.float32).T
    with scope("E_lowerw"):
        lower_pair.wait_recv()
    with scope("F_xw"):
        loads[7].wait()
        await_bytes(x_all.at[pl.ds(0, 2 * n_row - 1)], x_recv.at[0])

    def x_turned(which):
        strips = x_all[pl.ds(which * n_row, n_row)].reshape(depth, wide)
        return [strips[k * block:(k + 1) * block].T for k in range(depth // block)]

    with scope("G_turn"):
        x_t = jnp.concatenate(x_turned(side) + x_turned(other), axis=1)

    def part_copy(j, dh, dp, dq):
        rows = pl.ds(pl.multiple_of(j * span + lax.rem(quota + dq, shares) * share, share), share)
        return pltpu.make_async_remote_copy(
            src_ref=part.at[dh * 2 + dp, rows], dst_ref=part_in.at[j, number(*back(dh, dp, dq))],
            send_sem=part_send.at[0], recv_sem=part_recv.at[j],
            device_id=peer(dh, dp, dq), device_id_type=MESH,
        )

    for dh in reversed(range(halves)):
        for dp in reversed(range(2)):
            with scope(f"H_mm{dh}{dp}"):
                b = lax.rem(half + dh, halves) * 2 + lax.rem(layer + dp, 2)
                rows = pl.ds(pl.multiple_of(b * block, block), block)
                total = dot_last(x_t, jnp.concatenate([lower_all[0, rows, :], lower_all[1, rows, :]], axis=1))
                if (dh, dp) == (0, 0):
                    held[...] = total
                if len(group) and (dh, dp) == group[0][:2]:
                    pl.semaphore_wait(near, sum(step[0] == 0 for step in straights))
                part[dh * 2 + dp] = total.astype(jnp.bfloat16)
                for step in group:
                    if step[:2] == (dh, dp):
                        part_copy(0, *step).start()
    for j in range(1, chunks):
        for step in group:
            part_copy(j, *step).start()

    own_block = half * 2 + parity

    def anc_copy(j, dh, dp, dq):
        place = anc_t.at[j, own_block, pl.ds(pl.multiple_of(quota * share, share), share)]
        return pltpu.make_async_remote_copy(
            src_ref=place, dst_ref=place,
            send_sem=anc_send.at[0], recv_sem=anc_recv.at[j * len(group) + number(*back(dh, dp, dq))],
            device_id=peer(dh, dp, dq), device_id_type=MESH,
        )

    def anc_arrival(j, dh, dp, dq):
        place = anc_t.at[j, own_block, pl.ds(0, share)]
        return await_bytes(place, anc_recv.at[j * len(group) + number(dh, dp, dq)])

    inverse = inv_all[chosen]
    for j in range(chunks):
        with scope(f"I{j}_partw"):
            await_bytes(part_in.at[j], part_recv.at[j])
        with scope(f"J{j}_solve"):
            rows = pl.ds(pl.multiple_of(j * span + quota * share, share), share)
            remain = rhs_t[rows, :] - held[rows, :]
            for index in range(len(group)):
                remain = remain - part_in[j, index].astype(jnp.float32)
            high = remain.astype(jnp.bfloat16)
            rest = remain - high.astype(jnp.float32)
            middle = rest.astype(jnp.bfloat16)
            low = (rest - middle.astype(jnp.float32)).astype(jnp.bfloat16)
            terms = dot_last(jnp.concatenate([high, middle, low], axis=0), inverse)
            solved = terms[:share] + (terms[share:2 * share] + terms[2 * share:])
            anc_t[j, own_block, pl.ds(pl.multiple_of(quota * share, share), share)] = solved.astype(jnp.bfloat16)
            for step in group:
                anc_copy(j, *step).start()
    with scope("K_upperw"):
        upper_pair.wait_recv()

    def fold_copy(j, dr, which):
        to_row = lax.rem(row + dr, n_row)
        return pltpu.make_async_remote_copy(
            src_ref=fold.at[j, which, to_row], dst_ref=fold_in.at[j, which * n_row + dr],
            send_sem=fold_send.at[0], recv_sem=fold_recv.at[j],
            device_id=(layer, to_row, partner if which else col), device_id_type=MESH,
        )

    anc_pair = [pair_copy(4 + j, anc_t.at[j, partner], anc_other.at[j]) for j in range(chunks)]
    blocks_down = upper_all.shape[1] // block
    strips = block // strip
    for j in range(chunks):
        totals = [[None] * blocks_down for _ in range(2)]
        for dh in range(halves):
            for dp in range(2):
                with scope(f"L{j}_ancw{dh}{dp}"):
                    for dq in range(shares):
                        if (dh, dp, dq) != (0, 0, 0):
                            anc_arrival(j, dh, dp, dq)
                with scope(f"M{j}_mm{dh}{dp}"):
                    b = lax.rem(half + dh, halves) * 2 + lax.rem(layer + dp, 2)
                    across = pl.ds(pl.multiple_of(b * block, block), block)
                    solved = anc_t[j, b]
                    for which in range(2):
                        for i in range(blocks_down):
                            term = dot_last(upper_all[which, i * block:(i + 1) * block, across], solved)
                            before = totals[which][i]
                            totals[which][i] = term if before is None else before + term
        with scope(f"N{j}_pack"):
            for which in range(2):
                for i in range(blocks_down):
                    for s in range(strips):
                        piece = totals[which][i][s * strip:(s + 1) * strip].reshape(chunks, strip // chunks, span)
                        fold[j, which, i * strips + s] = jnp.concatenate(
                            [piece[g] for g in range(chunks)], axis=1
                        ).astype(jnp.bfloat16)
            for dr in reversed(range(n_row)):
                for which in (0, 1) if dr else (1,):
                    fold_copy(j, dr, which).start()
            anc_pair[j].start()

    with scope("O_ancout"):
        for copy in anc_pair:
            copy.wait_recv()
        anc_out[:, columns(side)] = jnp.concatenate([anc_t[j, col] for j in range(chunks)], axis=0).T
        anc_out[:, columns(other)] = jnp.concatenate([anc_other[j] for j in range(chunks)], axis=0).T
    sums = []
    for j in range(chunks):
        with scope(f"P{j}_foldw"):
            await_bytes(fold_in.at[j, pl.ds(1, 2 * n_row - 1)], fold_recv.at[j])
        own = fold[j, 0, row].astype(jnp.float32)
        for dr in range(1, n_row):
            own = own + fold_in[j, dr].astype(jnp.float32)
        others = fold_in[j, n_row].astype(jnp.float32)
        for dr in range(1, n_row):
            others = others + fold_in[j, n_row + dr].astype(jnp.float32)
        sums.append((own, others))
    with scope("Q_out"):
        for which, target in enumerate((side, other)):
            correct = jnp.concatenate(
                [
                    jnp.concatenate([sums[j][which][:, g * span:(g + 1) * span] for j in range(chunks)], axis=1)
                    for g in range(chunks)
                ],
                axis=0,
            )
            new_leaves[0, :, columns(target)] = (leaf_v[:, columns(target)].astype(jnp.float32) - correct).astype(jnp.bfloat16)

    with scope("R_drain"):
        for copy in (lower_pair, upper_pair, rhs_pair, inv_pair, *anc_pair):
            copy.wait_send()
        await_bytes(x_all.at[pl.ds(0, 2 * n_row - 1)], x_send.at[0])
        await_bytes(part_in, part_send.at[0])
        await_bytes(part_in, anc_send.at[0])
        await_bytes(fold_in.at[:, pl.ds(1, 2 * n_row - 1)], fold_send.at[0])


def finish(leaves, anc, leaves_out, anc_out, sem):
    copies = [
        pltpu.make_async_copy(anc, anc_out, sem.at[0]),
        pltpu.make_async_copy(leaves, leaves_out, sem.at[1]),
    ]
    for copy in copies:
        copy.start()
    for copy in copies:
        copy.wait()


def shards(n_layer, n_row, n_col, leaf_sol, lower_blocks, lower_mask, upper_blocks, upper_mask, anc_rhs, diag_inv):
    block = diag_inv.shape[1]
    width = leaf_sol.shape[2]
    strip = leaf_sol.shape[1]
    chunks = 2
    wide = width // 2
    span = wide // chunks
    share = span // (n_layer // 2)
    peers = n_layer * n_col // 2 - 1
    bf16, f32 = jnp.bfloat16, jnp.float32
    anywhere = pl.BlockSpec(memory_space=pltpu.HBM)
    lower_marks = lower_mask.T
    vmem = pl.BlockSpec(memory_space=pltpu.VMEM)
    dma = lambda *sizes: [pltpu.SemaphoreType.DMA((size,)) for size in sizes]
    out_shape = (
        jax.ShapeDtypeStruct(leaf_sol.shape, bf16),
        jax.ShapeDtypeStruct(anc_rhs.shape, bf16),
    )
    results = pl.pallas_call(
        functools.partial(kernel, n_layer, n_row, n_col, chunks),
        out_shape=(pltpu.VMEM(leaf_sol.shape, bf16), pltpu.VMEM(anc_rhs.shape, bf16)),
        in_specs=[anywhere] * 7,
        out_specs=(vmem, vmem),
        scratch_shapes=[
            pltpu.SMEM(lower_marks.shape, jnp.int32),
            pltpu.SMEM(upper_mask.shape, jnp.int32),
            pltpu.VMEM((strip, width), bf16),
            pltpu.VMEM((2, *lower_blocks.shape), bf16),
            pltpu.VMEM((2, *upper_blocks.shape), bf16),
            pltpu.VMEM((2, block, wide), bf16),
            pltpu.VMEM((2, block, block), bf16),
            pltpu.VMEM((2 * n_row, strip, wide), bf16),
            pltpu.VMEM((wide, block), f32),
            pltpu.VMEM((wide, block), f32),
            pltpu.VMEM((n_col, wide, block), bf16),
            pltpu.VMEM((chunks, peers, share, block), bf16),
            pltpu.VMEM((chunks, n_col, span, block), bf16),
            pltpu.VMEM((chunks, span, block), bf16),
            pltpu.VMEM((chunks, 2, n_row, strip // chunks, wide), bf16),
            pltpu.VMEM((chunks, 2 * n_row, strip // chunks, wide), bf16),
            *dma(8, 4 + chunks, 4 + chunks, 1, 1, 1, chunks, 1, chunks * peers, 1, chunks),
            pltpu.SemaphoreType.REGULAR,
        ],
        compiler_params=pltpu.CompilerParams(
            collective_id=0, has_side_effects=True,
        ),
    )(leaf_sol, lower_blocks, lower_marks, upper_blocks, upper_mask, anc_rhs, diag_inv)
    anyplace = pl.BlockSpec(memory_space=pl.ANY)
    return pl.pallas_call(
        finish,
        out_shape=out_shape,
        in_specs=[anyplace] * 2,
        out_specs=(anyplace, anyplace),
        scratch_shapes=dma(2),
        compiler_params=pltpu.CompilerParams(vmem_limit_bytes=1024 * 1024),
    )(*results)


def solution(mesh):
    in_specs = (
        P(("layer", "col"), "row", None),
        P(("layer", "row"), "col"),
        P(("layer", "row"), "col"),
        P(("layer", "col"), "row"),
        P(("layer", "col"), "row"),
        P(("row", "col"), None),
        P(("row", "col"), None),
    )
    out_specs = (P(("layer", "col"), "row", None), P(("row", "col"), None))
    body = functools.partial(shards, mesh.shape["layer"], mesh.shape["row"], mesh.shape["col"])
    return jax.shard_map(body, mesh=mesh, in_specs=in_specs, out_specs=out_specs, check_vma=False)
```

```python
import contextlib
import functools

import jax
import jax.numpy as jnp
from jax import lax
from jax.experimental import pallas as pl
from jax.experimental.pallas import tpu as pltpu
from jax.sharding import PartitionSpec as P

MESH = pl.DeviceIdType.MESH
scope = lambda name: contextlib.nullcontext()


def dot_last(a, b):
    return lax.dot_general(a, b, (((1,), (1,)), ((), ())), preferred_element_type=jnp.float32)


def dot(a, b):
    return jnp.dot(a, b, preferred_element_type=jnp.float32)


def await_bytes(ref, sem):
    pltpu.make_async_copy(ref, ref, sem).wait()


def kernel(
    n_layer, n_row, n_col, chunks, waves,
    leaf, lower, lower_marks, upper, upper_marks, rhs, inv,
    new_leaves, anc_out,
    lower_mask, upper_mask, leaf_v, lower_v, lower_all, upper_all, rhs_all, inv_all, x_out, x_all, rhs_t,
    held, part, part_in, anc_t, anc_other, fold, fold_in,
    local_sem, pair_send, pair_recv, x_send, x_recv, part_send, part_recv,
    anc_send, anc_recv, fold_send, fold_recv, near, higher,
):
    layer = lax.axis_index("layer")
    row = lax.axis_index("row")
    col = lax.axis_index("col")
    halves = n_col // 2
    shares = n_layer // 2
    half, side = col // 2, lax.rem(col, 2)
    other = 1 - side
    partner = half * 2 + other
    parity, quota = lax.rem(layer, 2), layer // 2
    block = inv.shape[0]
    strip, width = leaf_v.shape
    wide = width // 2
    span = wide // chunks
    share = span // shares
    batch = wide // waves
    pack = wide // strip
    depth = n_row * strip
    group = [
        (dh, dp, dq) for dh in reversed(range(halves)) for dp in reversed(range(2)) for dq in reversed(range(shares))
    ][:-1]

    def number(dh, dp, dq):
        return (dh * 2 + dp) * shares + dq - 1

    def back(dh, dp, dq):
        return (halves - dh) % halves, dp, (shares - dq) % shares

    def peer(dh, dp, dq):
        to_layer = lax.rem(quota + dq, shares) * 2 + lax.rem(layer + dp, 2)
        return to_layer, row, lax.rem(half + dh, halves) * 2 + side

    def straight(dh, dp, dq):
        return dh == 0 or (dp, dq) == (0, 0)

    barrier = pltpu.get_barrier_semaphore()

    def greet(*device):
        pl.semaphore_signal(barrier, inc=1, device_id=device, device_id_type=MESH)

    def above(step):
        return pl.when(row + step < n_row)

    def below(step):
        return pl.when(row >= step)

    for step in reversed(range(1, n_row)):
        @above(step)
        def _():
            greet(layer, row + step, col)
            greet(layer, row + step, partner)

    @below(1)
    def _():
        greet(layer, row - 1, col)
        greet(layer, row - 1, partner)

    greet(layer, row, partner)
    straights = [step for step in group if straight(*step)]
    for step in straights:
        greet(*peer(*step))

    def columns(which):
        return pl.ds(pl.multiple_of(which * wide, wide), wide)

    loads = [
        pltpu.make_async_copy(source, target, local_sem.at[index])
        for index, (source, target) in enumerate(
            (
                (lower_marks, lower_mask), (lower, lower_v), (upper_marks, upper_mask), (upper, upper_all.at[0]),
                (rhs.at[:, columns(side)], rhs_all.at[0]), (inv, inv_all.at[0]), (leaf.at[0], leaf_v),
            )
        )
    ]
    for load in reversed(loads):
        load.start()
    with scope("A_leaf"):
        loads[6].wait()
        turned = leaf_v[...].T
        for to_side in range(2):
            for w in range(waves):
                start = to_side * wide + w * batch
                pieces = [turned[start + g * (batch // pack):start + (g + 1) * (batch // pack)] for g in range(pack)]
                x_out[to_side, w] = jnp.concatenate(pieces, axis=1)
        for w in range(waves):
            x_all[w, side * n_row + row] = x_out[side, w]
    with scope("A_bar"):
        pl.semaphore_wait(barrier, 2 * row + 2 * jnp.minimum(n_row - 1 - row, 1) + 1 + len(straights))

    def x_copy(w, to_row, to_side, sem):
        return pltpu.make_async_remote_copy(
            src_ref=x_out.at[to_side, w], dst_ref=x_all.at[w, side * n_row + row],
            send_sem=x_send.at[0], recv_sem=x_recv.at[2 * w + sem],
            device_id=(layer, to_row, half * 2 + to_side), device_id_type=MESH,
        )

    def x_relay(w, from_side, step):
        place = x_all.at[w, from_side * n_row + jnp.maximum(row - 1, 0)]
        return pltpu.make_async_remote_copy(
            src_ref=place, dst_ref=place, send_sem=x_send.at[1], recv_sem=x_recv.at[2 * w + 1],
            device_id=(layer, row + step, col), device_id_type=MESH,
        )

    for w in range(waves):
        for step in reversed(range(1, n_row)):
            @below(step)
            def _():
                x_copy(w, row - step, side, 1).start()
                x_copy(w, row - step, other, 1).start()

        @above(1)
        def _():
            x_copy(w, row + 1, side, 0).start()
            x_copy(w, row + 1, other, 0).start()

        x_copy(w, row, other, 1).start()

    def tell_below():
        pl.semaphore_signal(higher, inc=1, device_id=(layer, row - 1, col), device_id_type=MESH)

    @pl.when((row >= 1) & (row < n_row - 1))
    def _():
        tell_below()

    def pair_copy(index, source, target):
        return pltpu.make_async_remote_copy(
            src_ref=source, dst_ref=target, send_sem=pair_send.at[index], recv_sem=pair_recv.at[index],
            device_id=(layer, row, partner), device_id_type=MESH,
        )

    lower_pair = pair_copy(0, lower_all.at[0], lower_all.at[1])
    upper_pair = pair_copy(1, upper_all.at[0], upper_all.at[1])
    rhs_pair = pair_copy(2, rhs.at[:, columns(other)], rhs_all.at[1])
    inv_pair = pair_copy(3, inv, inv_all.at[1])
    rhs_pair.start()
    inv_pair.start()
    for step in straights:
        if step[0] == 0:
            pl.semaphore_signal(near, inc=1, device_id=peer(*step), device_id_type=MESH)

    def marked(tile, mark):
        return tile * jnp.full((block, block), mark.astype(jnp.float32)).astype(jnp.bfloat16)

    def blocks_of(ref):
        rows, across = ref.shape
        return [(down, over) for down in range(rows // block) for over in range(across // block)]

    def at(down, over):
        return slice(down * block, (down + 1) * block), slice(over * block, (over + 1) * block)

    with scope("B_lower"):
        loads[0].wait()
        loads[1].wait()
        for down, over in blocks_of(lower_v):
            lower_all[(0, *at(over, down))] = marked(lower_v[at(down, over)], lower_mask[over, down]).T
        lower_pair.start()
    with scope("C_upper"):
        loads[2].wait()
        loads[3].wait()
        for down, over in blocks_of(upper):
            place = (0, *at(down, over))
            upper_all[place] = marked(upper_all[place], upper_mask[down, over])
        upper_pair.start()
    def relay(w, step):
        @pl.when((row >= 1) & (row + step < n_row))
        def _():
            for from_side in range(2):
                x_relay(w, from_side, step).start()

    for w in range(waves):
        with scope(f"D_relay{w}"):
            @below(1)
            def _():
                await_bytes(x_all.at[w, pl.ds(0, 2)], x_recv.at[2 * w])

            relay(w, 1)
            for step in range(2, n_row):
                if w == 0:
                    @above(step)
                    def _():
                        pl.semaphore_wait(higher, 1)

                        @below(1)
                        def _():
                            tell_below()

                relay(w, step)

    with scope("D_rhs"):
        loads[4].wait()
        loads[5].wait()
        rhs_pair.wait_recv()
        inv_pair.wait_recv()
        chosen = lax.rem(layer + side, 2)
        rhs_t[...] = rhs_all[chosen].astype(jnp.float32).T
    with scope("E_lowerw"):
        lower_pair.wait_recv()
    def x_turned(w, which):
        strips = x_all[w, pl.ds(which * n_row, n_row)]
        pieces = [
            jnp.concatenate([strips[r][:, g * strip:(g + 1) * strip] for g in range(pack)], axis=0)
            for r in range(n_row)
        ]
        return jnp.concatenate(pieces, axis=1)

    def part_copy(j, dh, dp, dq):
        rows = pl.ds(pl.multiple_of(j * span + lax.rem(quota + dq, shares) * share, share), share)
        return pltpu.make_async_remote_copy(
            src_ref=part.at[dh * 2 + dp, rows], dst_ref=part_in.at[j, number(*back(dh, dp, dq))],
            send_sem=part_send.at[0], recv_sem=part_recv.at[j],
            device_id=peer(dh, dp, dq), device_id_type=MESH,
        )

    def product(x_own, x_else, dh, dp):
        b = lax.rem(half + dh, halves) * 2 + lax.rem(layer + dp, 2)
        across = pl.ds(pl.multiple_of(b * block, block), block)
        return dot(x_own, lower_all[0, :, across]) + dot(x_else, lower_all[1, :, across])

    near_count = sum(step[0] == 0 for step in straights)
    x_t = []
    for w in range(waves):
        with scope(f"F{w}_xw"):
            for r in range(n_row):
                @pl.when(row == r)
                def _():
                    await_bytes(x_all.at[w, pl.ds(0, 2 * n_row - 1 - (2 if r else 0))], x_recv.at[2 * w + 1])
        with scope(f"G{w}_turn"):
            x_t.append((x_turned(w, side), x_turned(w, other)))
        within = range(w * (chunks // waves), (w + 1) * (chunks // waves))
        for dh in reversed(range(halves)):
            for dp in reversed(range(2)):
                if (dh, dp) == (0, 0):
                    continue
                with scope(f"H{w}_mm{dh}{dp}"):
                    part[dh * 2 + dp, w * batch:(w + 1) * batch] = product(*x_t[w], dh, dp).astype(jnp.bfloat16)
                    if w == 0 and (dh, dp) == group[0][:2]:
                        pl.semaphore_wait(near, near_count)
                    for step in group:
                        if step[:2] == (dh, dp):
                            part_copy(within[0], *step).start()
        for j in within[1:]:
            for step in group:
                if step[:2] != (0, 0):
                    part_copy(j, *step).start()
    with scope("H_own"):
        held[...] = product(*(jnp.concatenate(x, axis=0) for x in zip(*x_t)), 0, 0)
        if shares > 1:
            part[0] = held[...].astype(jnp.bfloat16)
            for j in range(chunks):
                for step in group:
                    if step[:2] == (0, 0):
                        part_copy(j, *step).start()

    own_block = half * 2 + parity

    def anc_copy(j, dh, dp, dq):
        place = anc_t.at[j, own_block, pl.ds(pl.multiple_of(quota * share, share), share)]
        return pltpu.make_async_remote_copy(
            src_ref=place, dst_ref=place,
            send_sem=anc_send.at[0], recv_sem=anc_recv.at[j],
            device_id=peer(dh, dp, dq), device_id_type=MESH,
        )

    inverse = inv_all[chosen]
    for j in range(chunks):
        with scope(f"I{j}_partw"):
            await_bytes(part_in.at[j], part_recv.at[j])
        with scope(f"J{j}_solve"):
            rows = pl.ds(pl.multiple_of(j * span + quota * share, share), share)
            remain = rhs_t[rows, :] - held[rows, :]
            for index in range(len(group)):
                remain = remain - part_in[j, index].astype(jnp.float32)
            high = remain.astype(jnp.bfloat16)
            rest = remain - high.astype(jnp.float32)
            middle = rest.astype(jnp.bfloat16)
            low = (rest - middle.astype(jnp.float32)).astype(jnp.bfloat16)
            terms = dot_last(jnp.concatenate([high, middle, low], axis=0), inverse)
            solved = terms[:share] + (terms[share:2 * share] + terms[2 * share:])
            anc_t[j, own_block, pl.ds(pl.multiple_of(quota * share, share), share)] = solved.astype(jnp.bfloat16)
            for step in group:
                anc_copy(j, *step).start()
    with scope("K_upperw"):
        upper_pair.wait_recv()

    def fold_copy(j, dr, which):
        to_row = lax.rem(row + dr, n_row)
        return pltpu.make_async_remote_copy(
            src_ref=fold.at[j, which, to_row], dst_ref=fold_in.at[j, which * n_row + dr],
            send_sem=fold_send.at[0], recv_sem=fold_recv.at[j],
            device_id=(layer, to_row, partner if which else col), device_id_type=MESH,
        )

    anc_pair = [pair_copy(4, anc_t.at[j, partner], anc_other.at[j]) for j in range(chunks)]
    blocks_down = upper_all.shape[1] // block
    strips = block // strip
    for j in range(chunks):
        with scope(f"L{j}_ancw"):
            await_bytes(part_in.at[j], anc_recv.at[j])
        with scope(f"M{j}_mm"):
            solved = jnp.concatenate([anc_t[j, b] for b in range(n_col)], axis=1)
            totals = [
                [dot_last(upper_all[which, i * block:(i + 1) * block, :], solved) for i in range(blocks_down)]
                for which in range(2)
            ]
        with scope(f"N{j}_pack"):
            for which in range(2):
                for i in range(blocks_down):
                    for s in range(strips):
                        piece = totals[which][i][s * strip:(s + 1) * strip].reshape(chunks, strip // chunks, span)
                        fold[j, which, i * strips + s] = jnp.concatenate(
                            [piece[g] for g in range(chunks)], axis=1
                        ).astype(jnp.bfloat16)
            for dr in reversed(range(n_row)):
                for which in (0, 1) if dr else (1,):
                    fold_copy(j, dr, which).start()
            anc_pair[j].start()

    with scope("O_ancout"):
        await_bytes(anc_other, pair_recv.at[4])
        anc_out[:, columns(side)] = jnp.concatenate([anc_t[j, col] for j in range(chunks)], axis=0).T
        anc_out[:, columns(other)] = jnp.concatenate([anc_other[j] for j in range(chunks)], axis=0).T
    sums = []
    for j in range(chunks):
        with scope(f"P{j}_foldw"):
            await_bytes(fold_in.at[j, pl.ds(1, 2 * n_row - 1)], fold_recv.at[j])
        own = fold[j, 0, row].astype(jnp.float32)
        for dr in range(1, n_row):
            own = own + fold_in[j, dr].astype(jnp.float32)
        others = fold_in[j, n_row].astype(jnp.float32)
        for dr in range(1, n_row):
            others = others + fold_in[j, n_row + dr].astype(jnp.float32)
        sums.append((own, others))
    with scope("Q_out"):
        for which, target in enumerate((side, other)):
            correct = jnp.concatenate(
                [
                    jnp.concatenate([sums[j][which][:, g * span:(g + 1) * span] for j in range(chunks)], axis=1)
                    for g in range(chunks)
                ],
                axis=0,
            )
            new_leaves[0, :, columns(target)] = (leaf_v[:, columns(target)].astype(jnp.float32) - correct).astype(jnp.bfloat16)

    with scope("R_drain"):
        for copy in (lower_pair, upper_pair, rhs_pair, inv_pair):
            copy.wait_send()
        await_bytes(anc_other, pair_send.at[4])
        for r in range(n_row):
            @pl.when(row == r)
            def _():
                await_bytes(x_all.at[:, pl.ds(0, 2 * r + 1 + (2 if r < n_row - 1 else 0))], x_send.at[0])
                if 0 < r < n_row - 1:
                    await_bytes(x_all.at[:, pl.ds(0, 2 * (n_row - 1 - r))], x_send.at[1])

        await_bytes(part_in, part_send.at[0])
        await_bytes(part_in, anc_send.at[0])
        await_bytes(fold_in.at[:, pl.ds(1, 2 * n_row - 1)], fold_send.at[0])


def finish(leaves, anc, leaves_out, anc_out, sem):
    copies = [
        pltpu.make_async_copy(anc, anc_out, sem.at[0]),
        pltpu.make_async_copy(leaves, leaves_out, sem.at[1]),
    ]
    for copy in copies:
        copy.start()
    for copy in copies:
        copy.wait()


def shards(n_layer, n_row, n_col, leaf_sol, lower_blocks, lower_mask, upper_blocks, upper_mask, anc_rhs, diag_inv):
    block = diag_inv.shape[1]
    width = leaf_sol.shape[2]
    strip = leaf_sol.shape[1]
    chunks, waves = 4, 2
    wide = width // 2
    span = wide // chunks
    share = span // (n_layer // 2)
    peers = n_layer * n_col // 2 - 1
    bf16, f32 = jnp.bfloat16, jnp.float32
    anywhere = pl.BlockSpec(memory_space=pltpu.HBM)
    lower_marks = lower_mask.T
    vmem = pl.BlockSpec(memory_space=pltpu.VMEM)
    dma = lambda *sizes: [pltpu.SemaphoreType.DMA((size,)) for size in sizes]
    out_shape = (
        jax.ShapeDtypeStruct(leaf_sol.shape, bf16),
        jax.ShapeDtypeStruct(anc_rhs.shape, bf16),
    )
    results = pl.pallas_call(
        functools.partial(kernel, n_layer, n_row, n_col, chunks, waves),
        out_shape=(pltpu.VMEM(leaf_sol.shape, bf16), pltpu.VMEM(anc_rhs.shape, bf16)),
        in_specs=[anywhere] * 7,
        out_specs=(vmem, vmem),
        scratch_shapes=[
            pltpu.SMEM(lower_marks.shape, jnp.int32),
            pltpu.SMEM(upper_mask.shape, jnp.int32),
            pltpu.VMEM((strip, width), bf16),
            pltpu.VMEM(lower_blocks.shape, bf16),
            pltpu.VMEM((2, *lower_blocks.shape[::-1]), bf16),
            pltpu.VMEM((2, *upper_blocks.shape), bf16),
            pltpu.VMEM((2, block, wide), bf16),
            pltpu.VMEM((2, block, block), bf16),
            pltpu.VMEM((2, waves, strip // waves, wide), bf16),
            pltpu.VMEM((waves, 2 * n_row, strip // waves, wide), bf16),
            pltpu.VMEM((wide, block), f32),
            pltpu.VMEM((wide, block), f32),
            pltpu.VMEM((n_col, wide, block), bf16),
            pltpu.VMEM((chunks, peers, share, block), bf16),
            pltpu.VMEM((chunks, n_col, span, block), bf16),
            pltpu.VMEM((chunks, span, block), bf16),
            pltpu.VMEM((chunks, 2, n_row, strip // chunks, wide), bf16),
            pltpu.VMEM((chunks, 2 * n_row, strip // chunks, wide), bf16),
            *dma(7, 5, 5, 2, 2 * waves, 1, chunks, 1, chunks, 1, chunks),
            pltpu.SemaphoreType.REGULAR,
            pltpu.SemaphoreType.REGULAR,
        ],
        compiler_params=pltpu.CompilerParams(
            collective_id=0, has_side_effects=True,
        ),
    )(leaf_sol, lower_blocks, lower_marks, upper_blocks, upper_mask, anc_rhs, diag_inv)
    anyplace = pl.BlockSpec(memory_space=pl.ANY)
    return pl.pallas_call(
        finish,
        out_shape=out_shape,
        in_specs=[anyplace] * 2,
        out_specs=(anyplace, anyplace),
        scratch_shapes=dma(2),
        compiler_params=pltpu.CompilerParams(vmem_limit_bytes=1024 * 1024),
    )(*results)


def solution(mesh):
    in_specs = (
        P(("layer", "col"), "row", None),
        P(("layer", "row"), "col"),
        P(("layer", "row"), "col"),
        P(("layer", "col"), "row"),
        P(("layer", "col"), "row"),
        P(("row", "col"), None),
        P(("row", "col"), None),
    )
    out_specs = (P(("layer", "col"), "row", None), P(("row", "col"), None))
    body = functools.partial(shards, mesh.shape["layer"], mesh.shape["row"], mesh.shape["col"])
    return jax.shard_map(body, mesh=mesh, in_specs=in_specs, out_specs=out_specs, check_vma=False)
```

```python
import contextlib
import functools

import jax
import jax.numpy as jnp
from jax import lax
from jax.experimental import pallas as pl
from jax.experimental.pallas import tpu as pltpu
from jax.sharding import PartitionSpec as P

MESH = pl.DeviceIdType.MESH
scope = lambda name: contextlib.nullcontext()


def dot_last(a, b):
    return lax.dot_general(a, b, (((1,), (1,)), ((), ())), preferred_element_type=jnp.float32)


def dot(a, b):
    return jnp.dot(a, b, preferred_element_type=jnp.float32)


def await_bytes(ref, sem):
    pltpu.make_async_copy(ref, ref, sem).wait()


def kernel(
    n_layer, n_row, n_col, chunks, waves,
    leaf, lower, lower_marks, upper, upper_marks, rhs, inv,
    new_leaves, anc_out,
    lower_mask, upper_mask, leaf_v, lower_v, lower_all, upper_all, rhs_all, inv_all, x_out, x_all, rhs_t,
    held, part, part_in, anc_t, anc_other, fold, fold_in,
    local_sem, pair_send, pair_recv, x_send, x_recv, part_send, part_recv,
    anc_send, anc_recv, fold_send, fold_recv, near, higher,
):
    layer = lax.axis_index("layer")
    row = lax.axis_index("row")
    col = lax.axis_index("col")
    halves = n_col // 2
    shares = n_layer // 2
    half, side = col // 2, lax.rem(col, 2)
    other = 1 - side
    partner = half * 2 + other
    parity, quota = lax.rem(layer, 2), layer // 2
    block = inv.shape[0]
    strip, width = leaf_v.shape
    wide = width // 2
    span = wide // chunks
    share = span // shares
    batch = wide // waves
    pack = wide // strip
    depth = n_row * strip
    group = [
        (dh, dp, dq) for dh in reversed(range(halves)) for dp in reversed(range(2)) for dq in reversed(range(shares))
    ][:-1]

    def number(dh, dp, dq):
        return (dh * 2 + dp) * shares + dq - 1

    def back(dh, dp, dq):
        return (halves - dh) % halves, dp, (shares - dq) % shares

    def peer(dh, dp, dq):
        to_layer = lax.rem(quota + dq, shares) * 2 + lax.rem(layer + dp, 2)
        return to_layer, row, lax.rem(half + dh, halves) * 2 + side

    def straight(dh, dp, dq):
        return dh == 0 or (dp, dq) == (0, 0)

    barrier = pltpu.get_barrier_semaphore()

    def greet(*device):
        pl.semaphore_signal(barrier, inc=1, device_id=device, device_id_type=MESH)

    def above(step):
        return pl.when(row + step < n_row)

    def below(step):
        return pl.when(row >= step)

    for step in reversed(range(1, n_row)):
        @above(step)
        def _():
            greet(layer, row + step, col)
            greet(layer, row + step, partner)

    @below(1)
    def _():
        greet(layer, row - 1, col)
        greet(layer, row - 1, partner)

    greet(layer, row, partner)
    straights = [step for step in group if straight(*step)]
    for step in straights:
        greet(*peer(*step))

    def columns(which):
        return pl.ds(pl.multiple_of(which * wide, wide), wide)

    loads = [
        pltpu.make_async_copy(source, target, local_sem.at[index])
        for index, (source, target) in enumerate(
            (
                (lower_marks, lower_mask), (lower, lower_v), (upper_marks, upper_mask), (upper, upper_all.at[0]),
                (rhs.at[:, columns(side)], rhs_all.at[0]), (inv, inv_all.at[0]), (leaf.at[0], leaf_v),
            )
        )
    ]
    for load in reversed(loads):
        load.start()
    with scope("A_leaf"):
        loads[6].wait()
        turned = leaf_v[...].T
        for to_side in range(2):
            for w in range(waves):
                start = to_side * wide + w * batch
                pieces = [turned[start + g * (batch // pack):start + (g + 1) * (batch // pack)] for g in range(pack)]
                x_out[to_side, w] = jnp.concatenate(pieces, axis=1)
        for w in range(waves):
            x_all[w, side * n_row + row] = x_out[side, w]
    with scope("A_bar"):
        pl.semaphore_wait(barrier, 2 * row + 2 * jnp.minimum(n_row - 1 - row, 1) + 1 + len(straights))

    def x_copy(w, to_row, to_side, sem):
        return pltpu.make_async_remote_copy(
            src_ref=x_out.at[to_side, w], dst_ref=x_all.at[w, side * n_row + row],
            send_sem=x_send.at[0], recv_sem=x_recv.at[2 * w + sem],
            device_id=(layer, to_row, half * 2 + to_side), device_id_type=MESH,
        )

    def x_relay(w, from_side, step):
        place = x_all.at[w, from_side * n_row + jnp.maximum(row - 1, 0)]
        return pltpu.make_async_remote_copy(
            src_ref=place, dst_ref=place, send_sem=x_send.at[1], recv_sem=x_recv.at[2 * w + 1],
            device_id=(layer, row + step, col), device_id_type=MESH,
        )

    for w in range(waves):
        for step in reversed(range(1, n_row)):
            @below(step)
            def _():
                x_copy(w, row - step, side, 1).start()
                x_copy(w, row - step, other, 1).start()

        @above(1)
        def _():
            x_copy(w, row + 1, side, 0).start()
            x_copy(w, row + 1, other, 0).start()

        x_copy(w, row, other, 1).start()

    def tell_below():
        pl.semaphore_signal(higher, inc=1, device_id=(layer, row - 1, col), device_id_type=MESH)

    @pl.when((row >= 1) & (row < n_row - 1))
    def _():
        tell_below()

    def pair_copy(index, source, target):
        return pltpu.make_async_remote_copy(
            src_ref=source, dst_ref=target, send_sem=pair_send.at[index], recv_sem=pair_recv.at[index],
            device_id=(layer, row, partner), device_id_type=MESH,
        )

    lower_pair = pair_copy(0, lower_all.at[0], lower_all.at[1])
    upper_pair = pair_copy(1, upper_all.at[0], upper_all.at[1])
    rhs_pair = pair_copy(2, rhs.at[:, columns(other)], rhs_all.at[1])
    inv_pair = pair_copy(3, inv, inv_all.at[1])
    for step in straights:
        if step[0] == 0:
            pl.semaphore_signal(near, inc=1, device_id=peer(*step), device_id_type=MESH)

    def marked(tile, mark):
        return tile * jnp.full((block, block), mark.astype(jnp.float32)).astype(jnp.bfloat16)

    def blocks_of(ref):
        rows, across = ref.shape
        return [(down, over) for down in range(rows // block) for over in range(across // block)]

    def at(down, over):
        return slice(down * block, (down + 1) * block), slice(over * block, (over + 1) * block)

    with scope("B_lower"):
        loads[0].wait()
        loads[1].wait()
        for down, over in blocks_of(lower_v):
            lower_all[(0, *at(over, down))] = marked(lower_v[at(down, over)], lower_mask[over, down]).T
        lower_pair.start()
    with scope("C_upper"):
        loads[2].wait()
        loads[3].wait()
        for down, over in blocks_of(upper):
            place = (0, *at(down, over))
            upper_all[place] = marked(upper_all[place], upper_mask[down, over])
    def relay(w, step):
        @pl.when((row >= 1) & (row + step < n_row))
        def _():
            for from_side in range(2):
                x_relay(w, from_side, step).start()

    for w in range(waves):
        with scope(f"D_relay{w}"):
            @below(1)
            def _():
                await_bytes(x_all.at[w, pl.ds(0, 2)], x_recv.at[2 * w])

            relay(w, 1)
            for step in range(2, n_row):
                if w == 0:
                    @above(step)
                    def _():
                        pl.semaphore_wait(higher, 1)

                        @below(1)
                        def _():
                            tell_below()

                relay(w, step)

    with scope("D_rhs"):
        loads[4].wait()
        loads[5].wait()
        chosen = lax.rem(layer + side, 2)
    with scope("E_lowerw"):
        lower_pair.wait_recv()
    def x_turned(w, which):
        strips = x_all[w, pl.ds(which * n_row, n_row)]
        pieces = [
            jnp.concatenate([strips[r][:, g * strip:(g + 1) * strip] for g in range(pack)], axis=0)
            for r in range(n_row)
        ]
        return jnp.concatenate(pieces, axis=1)

    def part_copy(j, dh, dp, dq):
        rows = pl.ds(pl.multiple_of(j * span + lax.rem(quota + dq, shares) * share, share), share)
        return pltpu.make_async_remote_copy(
            src_ref=part.at[dh * 2 + dp, rows], dst_ref=part_in.at[j, number(*back(dh, dp, dq))],
            send_sem=part_send.at[0], recv_sem=part_recv.at[j],
            device_id=peer(dh, dp, dq), device_id_type=MESH,
        )

    def product(x_own, x_else, dh, dp):
        b = lax.rem(half + dh, halves) * 2 + lax.rem(layer + dp, 2)
        across = pl.ds(pl.multiple_of(b * block, block), block)
        return dot(x_own, lower_all[0, :, across]) + dot(x_else, lower_all[1, :, across])

    near_count = sum(step[0] == 0 for step in straights)
    x_t, later = [], ()
    for w in range(waves):
        with scope(f"F{w}_xw"):
            for r in range(n_row):
                @pl.when(row == r)
                def _():
                    await_bytes(x_all.at[w, pl.ds(0, 2 * n_row - 1 - (2 if r else 0))], x_recv.at[2 * w + 1])
        with scope(f"G{w}_turn"):
            x_t.append((x_turned(w, side), x_turned(w, other)))
        within = range(w * (chunks // waves), (w + 1) * (chunks // waves))
        for j in later:
            for step in group:
                if step[:2] != (0, 0):
                    part_copy(j, *step).start()
        later = within[1:]
        for dh in reversed(range(halves)):
            for dp in reversed(range(2)):
                if (dh, dp) == (0, 0):
                    continue
                with scope(f"H{w}_mm{dh}{dp}"):
                    part[dh * 2 + dp, w * batch:(w + 1) * batch] = product(*x_t[w], dh, dp).astype(jnp.bfloat16)
                    if w == 0 and (dh, dp) == group[0][:2]:
                        pl.semaphore_wait(near, near_count)
                    for step in group:
                        if step[:2] == (dh, dp):
                            part_copy(within[0], *step).start()
    for j in later:
        for step in group:
            if step[:2] != (0, 0):
                part_copy(j, *step).start()
    rhs_pair.start()
    inv_pair.start()
    upper_pair.start()
    with scope("H_own"):
        held[...] = product(*(jnp.concatenate(x, axis=0) for x in zip(*x_t)), 0, 0)
        if shares > 1:
            part[0] = held[...].astype(jnp.bfloat16)
            for j in range(chunks):
                for step in group:
                    if step[:2] == (0, 0):
                        part_copy(j, *step).start()

    own_block = half * 2 + parity

    def anc_copy(j, dh, dp, dq):
        place = anc_t.at[j, own_block, pl.ds(pl.multiple_of(quota * share, share), share)]
        return pltpu.make_async_remote_copy(
            src_ref=place, dst_ref=place,
            send_sem=anc_send.at[0], recv_sem=anc_recv.at[j],
            device_id=peer(dh, dp, dq), device_id_type=MESH,
        )

    with scope("H_rhs"):
        rhs_pair.wait_recv()
        inv_pair.wait_recv()
        rhs_t[...] = rhs_all[chosen].astype(jnp.float32).T
    inverse = inv_all[chosen]
    for j in range(chunks):
        with scope(f"I{j}_partw"):
            await_bytes(part_in.at[j], part_recv.at[j])
        with scope(f"J{j}_solve"):
            rows = pl.ds(pl.multiple_of(j * span + quota * share, share), share)
            remain = rhs_t[rows, :] - held[rows, :]
            for index in range(len(group)):
                remain = remain - part_in[j, index].astype(jnp.float32)
            high = remain.astype(jnp.bfloat16)
            rest = remain - high.astype(jnp.float32)
            middle = rest.astype(jnp.bfloat16)
            low = (rest - middle.astype(jnp.float32)).astype(jnp.bfloat16)
            terms = dot_last(jnp.concatenate([high, middle, low], axis=0), inverse)
            solved = terms[:share] + (terms[share:2 * share] + terms[2 * share:])
            anc_t[j, own_block, pl.ds(pl.multiple_of(quota * share, share), share)] = solved.astype(jnp.bfloat16)
            for step in group:
                anc_copy(j, *step).start()
    with scope("K_upperw"):
        upper_pair.wait_recv()

    def fold_copy(j, dr, which):
        to_row = lax.rem(row + dr, n_row)
        return pltpu.make_async_remote_copy(
            src_ref=fold.at[j, which, to_row], dst_ref=fold_in.at[j, which * n_row + dr],
            send_sem=fold_send.at[0], recv_sem=fold_recv.at[j],
            device_id=(layer, to_row, partner if which else col), device_id_type=MESH,
        )

    anc_pair = [pair_copy(4, anc_t.at[j, partner], anc_other.at[j]) for j in range(chunks)]
    blocks_down = upper_all.shape[1] // block
    strips = block // strip
    for j in range(chunks):
        with scope(f"L{j}_ancw"):
            await_bytes(part_in.at[j], anc_recv.at[j])
        with scope(f"M{j}_mm"):
            solved = jnp.concatenate([anc_t[j, b] for b in range(n_col)], axis=1)
            totals = [
                [
                    dot_last(upper_all[which, i * block:(i + 1) * block, :], solved).astype(jnp.bfloat16)
                    for i in range(blocks_down)
                ]
                for which in range(2)
            ]
        with scope(f"N{j}_pack"):
            for which in range(2):
                for i in range(blocks_down):
                    for s in range(strips):
                        piece = totals[which][i][s * strip:(s + 1) * strip].reshape(chunks, strip // chunks, span)
                        fold[j, which, i * strips + s] = jnp.concatenate([piece[g] for g in range(chunks)], axis=1)
            for dr in reversed(range(n_row)):
                for which in (0, 1) if dr else (1,):
                    fold_copy(j, dr, which).start()
            anc_pair[j].start()

    with scope("O_ancout"):
        await_bytes(anc_other, pair_recv.at[4])
        anc_out[:, columns(side)] = jnp.concatenate([anc_t[j, col] for j in range(chunks)], axis=0).T
        anc_out[:, columns(other)] = jnp.concatenate([anc_other[j] for j in range(chunks)], axis=0).T
    sums = []
    for j in range(chunks):
        with scope(f"P{j}_foldw"):
            await_bytes(fold_in.at[j, pl.ds(1, 2 * n_row - 1)], fold_recv.at[j])
        own = fold[j, 0, row].astype(jnp.float32)
        for dr in range(1, n_row):
            own = own + fold_in[j, dr].astype(jnp.float32)
        others = fold_in[j, n_row].astype(jnp.float32)
        for dr in range(1, n_row):
            others = others + fold_in[j, n_row + dr].astype(jnp.float32)
        sums.append((own, others))
    with scope("Q_out"):
        for which, target in enumerate((side, other)):
            correct = jnp.concatenate(
                [
                    jnp.concatenate([sums[j][which][:, g * span:(g + 1) * span] for j in range(chunks)], axis=1)
                    for g in range(chunks)
                ],
                axis=0,
            )
            new_leaves[0, :, columns(target)] = (leaf_v[:, columns(target)].astype(jnp.float32) - correct).astype(jnp.bfloat16)

    with scope("R_drain"):
        for copy in (lower_pair, upper_pair, rhs_pair, inv_pair):
            copy.wait_send()
        await_bytes(anc_other, pair_send.at[4])
        for r in range(n_row):
            @pl.when(row == r)
            def _():
                await_bytes(x_all.at[:, pl.ds(0, 2 * r + 1 + (2 if r < n_row - 1 else 0))], x_send.at[0])
                if 0 < r < n_row - 1:
                    await_bytes(x_all.at[:, pl.ds(0, 2 * (n_row - 1 - r))], x_send.at[1])

        await_bytes(part_in, part_send.at[0])
        await_bytes(part_in, anc_send.at[0])
        await_bytes(fold_in.at[:, pl.ds(1, 2 * n_row - 1)], fold_send.at[0])


def finish(leaves, anc, leaves_out, anc_out, sem):
    copies = [
        pltpu.make_async_copy(anc, anc_out, sem.at[0]),
        pltpu.make_async_copy(leaves, leaves_out, sem.at[1]),
    ]
    for copy in copies:
        copy.start()
    for copy in copies:
        copy.wait()


def shards(n_layer, n_row, n_col, leaf_sol, lower_blocks, lower_mask, upper_blocks, upper_mask, anc_rhs, diag_inv):
    block = diag_inv.shape[1]
    width = leaf_sol.shape[2]
    strip = leaf_sol.shape[1]
    chunks, waves = 2, 2
    wide = width // 2
    span = wide // chunks
    share = span // (n_layer // 2)
    peers = n_layer * n_col // 2 - 1
    bf16, f32 = jnp.bfloat16, jnp.float32
    anywhere = pl.BlockSpec(memory_space=pltpu.HBM)
    lower_marks = lower_mask.T
    vmem = pl.BlockSpec(memory_space=pltpu.VMEM)
    dma = lambda *sizes: [pltpu.SemaphoreType.DMA((size,)) for size in sizes]
    out_shape = (
        jax.ShapeDtypeStruct(leaf_sol.shape, bf16),
        jax.ShapeDtypeStruct(anc_rhs.shape, bf16),
    )
    results = pl.pallas_call(
        functools.partial(kernel, n_layer, n_row, n_col, chunks, waves),
        out_shape=(pltpu.VMEM(leaf_sol.shape, bf16), pltpu.VMEM(anc_rhs.shape, bf16)),
        in_specs=[anywhere] * 7,
        out_specs=(vmem, vmem),
        scratch_shapes=[
            pltpu.SMEM(lower_marks.shape, jnp.int32),
            pltpu.SMEM(upper_mask.shape, jnp.int32),
            pltpu.VMEM((strip, width), bf16),
            pltpu.VMEM(lower_blocks.shape, bf16),
            pltpu.VMEM((2, *lower_blocks.shape[::-1]), bf16),
            pltpu.VMEM((2, *upper_blocks.shape), bf16),
            pltpu.VMEM((2, block, wide), bf16),
            pltpu.VMEM((2, block, block), bf16),
            pltpu.VMEM((2, waves, strip // waves, wide), bf16),
            pltpu.VMEM((waves, 2 * n_row, strip // waves, wide), bf16),
            pltpu.VMEM((wide, block), f32),
            pltpu.VMEM((wide, block), f32),
            pltpu.VMEM((n_col, wide, block), bf16),
            pltpu.VMEM((chunks, peers, share, block), bf16),
            pltpu.VMEM((chunks, n_col, span, block), bf16),
            pltpu.VMEM((chunks, span, block), bf16),
            pltpu.VMEM((chunks, 2, n_row, strip // chunks, wide), bf16),
            pltpu.VMEM((chunks, 2 * n_row, strip // chunks, wide), bf16),
            *dma(7, 5, 5, 2, 2 * waves, 1, chunks, 1, chunks, 1, chunks),
            pltpu.SemaphoreType.REGULAR,
            pltpu.SemaphoreType.REGULAR,
        ],
        compiler_params=pltpu.CompilerParams(
            collective_id=0, has_side_effects=True,
        ),
    )(leaf_sol, lower_blocks, lower_marks, upper_blocks, upper_mask, anc_rhs, diag_inv)
    anyplace = pl.BlockSpec(memory_space=pl.ANY)
    return pl.pallas_call(
        finish,
        out_shape=out_shape,
        in_specs=[anyplace] * 2,
        out_specs=(anyplace, anyplace),
        scratch_shapes=dma(2),
        compiler_params=pltpu.CompilerParams(vmem_limit_bytes=1024 * 1024),
    )(*results)


def solution(mesh):
    in_specs = (
        P(("layer", "col"), "row", None),
        P(("layer", "row"), "col"),
        P(("layer", "row"), "col"),
        P(("layer", "col"), "row"),
        P(("layer", "col"), "row"),
        P(("row", "col"), None),
        P(("row", "col"), None),
    )
    out_specs = (P(("layer", "col"), "row", None), P(("row", "col"), None))
    body = functools.partial(shards, mesh.shape["layer"], mesh.shape["row"], mesh.shape["col"])
    return jax.shard_map(body, mesh=mesh, in_specs=in_specs, out_specs=out_specs, check_vma=False)
```

```python
import contextlib
import functools

import jax
import jax.numpy as jnp
from jax import lax
from jax.experimental import pallas as pl
from jax.experimental.pallas import tpu as pltpu
from jax.sharding import PartitionSpec as P

MESH = pl.DeviceIdType.MESH
scope = lambda name: contextlib.nullcontext()


def dot_last(a, b):
    return lax.dot_general(a, b, (((1,), (1,)), ((), ())), preferred_element_type=jnp.float32)


def dot(a, b):
    return jnp.dot(a, b, preferred_element_type=jnp.float32)


def await_bytes(ref, sem):
    pltpu.make_async_copy(ref, ref, sem).wait()


def kernel(
    n_layer, n_row, n_col, chunks, waves,
    leaf, lower, lower_marks, upper, upper_marks, rhs, inv,
    new_leaves, anc_out,
    lower_mask, upper_mask, leaf_v, lower_v, lower_all, upper_all, rhs_all, inv_all, x_out, x_all, rhs_t,
    held, part, part_in, anc_t, anc_other, fold, fold_in,
    local_sem, pair_send, pair_recv, x_send, x_recv, part_send, part_recv,
    anc_send, anc_recv, fold_send, fold_recv, near, higher,
):
    layer = lax.axis_index("layer")
    row = lax.axis_index("row")
    col = lax.axis_index("col")
    halves = n_col // 2
    shares = n_layer // 2
    half, side = col // 2, lax.rem(col, 2)
    other = 1 - side
    partner = half * 2 + other
    parity, quota = lax.rem(layer, 2), layer // 2
    block = inv.shape[0]
    strip, width = leaf_v.shape
    wide = width // 2
    span = wide // chunks
    share = span // shares
    batch = wide // waves
    pack = wide // strip
    depth = n_row * strip
    group = [
        (dh, dp, dq) for dh in reversed(range(halves)) for dp in reversed(range(2)) for dq in reversed(range(shares))
    ][:-1]

    def number(dh, dp, dq):
        return (dh * 2 + dp) * shares + dq - 1

    def back(dh, dp, dq):
        return (halves - dh) % halves, dp, (shares - dq) % shares

    def peer(dh, dp, dq):
        to_layer = lax.rem(quota + dq, shares) * 2 + lax.rem(layer + dp, 2)
        return to_layer, row, lax.rem(half + dh, halves) * 2 + side

    def straight(dh, dp, dq):
        return dh == 0 or (dp, dq) == (0, 0)

    leaf_load = pltpu.make_async_copy(leaf.at[0], leaf_v, local_sem.at[6])
    leaf_load.start()
    barrier = pltpu.get_barrier_semaphore()

    def greet(*device):
        pl.semaphore_signal(barrier, inc=1, device_id=device, device_id_type=MESH)

    def above(step):
        return pl.when(row + step < n_row)

    def below(step):
        return pl.when(row >= step)

    for step in reversed(range(1, n_row)):
        @above(step)
        def _():
            greet(layer, row + step, col)
            greet(layer, row + step, partner)

    @below(1)
    def _():
        greet(layer, row - 1, col)
        greet(layer, row - 1, partner)

    greet(layer, row, partner)
    straights = [step for step in group if straight(*step)]
    for step in straights:
        greet(*peer(*step))

    def columns(which):
        return pl.ds(pl.multiple_of(which * wide, wide), wide)

    loads = [
        pltpu.make_async_copy(source, target, local_sem.at[index])
        for index, (source, target) in enumerate(
            (
                (lower_marks, lower_mask), (lower, lower_v), (upper_marks, upper_mask), (upper, upper_all.at[0]),
                (rhs.at[:, columns(side)], rhs_all.at[0]), (inv, inv_all.at[0]),
            )
        )
    ]
    for load in loads:
        load.start()
    with scope("A_leaf"):
        leaf_load.wait()
        turned = leaf_v[...].T
        for to_side in range(2):
            for w in range(waves):
                start = to_side * wide + w * batch
                pieces = [turned[start + g * (batch // pack):start + (g + 1) * (batch // pack)] for g in range(pack)]
                x_out[to_side, w] = jnp.concatenate(pieces, axis=1)
        for w in range(waves):
            x_all[w, side * n_row + row] = x_out[side, w]
    with scope("A_bar"):
        pl.semaphore_wait(barrier, 2 * row + 2 * jnp.minimum(n_row - 1 - row, 1) + 1 + len(straights))

    def x_copy(w, to_row, to_side, sem):
        return pltpu.make_async_remote_copy(
            src_ref=x_out.at[to_side, w], dst_ref=x_all.at[w, side * n_row + row],
            send_sem=x_send.at[0], recv_sem=x_recv.at[2 * w + sem],
            device_id=(layer, to_row, half * 2 + to_side), device_id_type=MESH,
        )

    def x_relay(w, from_side, step):
        place = x_all.at[w, from_side * n_row + jnp.maximum(row - 1, 0)]
        return pltpu.make_async_remote_copy(
            src_ref=place, dst_ref=place, send_sem=x_send.at[1], recv_sem=x_recv.at[2 * w + 1],
            device_id=(layer, row + step, col), device_id_type=MESH,
        )

    for w in range(waves):
        for step in reversed(range(1, n_row)):
            @below(step)
            def _():
                x_copy(w, row - step, side, 1).start()
                x_copy(w, row - step, other, 1).start()

        @above(1)
        def _():
            x_copy(w, row + 1, side, 0).start()
            x_copy(w, row + 1, other, 0).start()

        x_copy(w, row, other, 1).start()

    def tell_below():
        pl.semaphore_signal(higher, inc=1, device_id=(layer, row - 1, col), device_id_type=MESH)

    @pl.when((row >= 1) & (row < n_row - 1))
    def _():
        tell_below()

    def pair_copy(index, source, target):
        return pltpu.make_async_remote_copy(
            src_ref=source, dst_ref=target, send_sem=pair_send.at[index], recv_sem=pair_recv.at[index],
            device_id=(layer, row, partner), device_id_type=MESH,
        )

    lower_pair = pair_copy(0, lower_all.at[0], lower_all.at[1])
    upper_pair = pair_copy(1, upper_all.at[0], upper_all.at[1])
    rhs_pair = pair_copy(2, rhs.at[:, columns(other)], rhs_all.at[1])
    inv_pair = pair_copy(3, inv, inv_all.at[1])
    for step in straights:
        if step[0] == 0:
            pl.semaphore_signal(near, inc=1, device_id=peer(*step), device_id_type=MESH)

    def marked(tile, mark):
        return tile * jnp.full((block, block), mark.astype(jnp.float32)).astype(jnp.bfloat16)

    def blocks_of(ref):
        rows, across = ref.shape
        return [(down, over) for down in range(rows // block) for over in range(across // block)]

    def at(down, over):
        return slice(down * block, (down + 1) * block), slice(over * block, (over + 1) * block)

    with scope("B_lower"):
        loads[0].wait()
        loads[1].wait()
        for down, over in blocks_of(lower_v):
            lower_all[(0, *at(over, down))] = marked(lower_v[at(down, over)], lower_mask[over, down]).T
        lower_pair.start()
    with scope("C_upper"):
        loads[2].wait()
        loads[3].wait()
        for down, over in blocks_of(upper):
            place = (0, *at(down, over))
            upper_all[place] = marked(upper_all[place], upper_mask[down, over])
    def relay(w, step):
        @pl.when((row >= 1) & (row + step < n_row))
        def _():
            for from_side in range(2):
                x_relay(w, from_side, step).start()

    for w in range(waves):
        with scope(f"D_relay{w}"):
            @below(1)
            def _():
                await_bytes(x_all.at[w, pl.ds(0, 2)], x_recv.at[2 * w])

            relay(w, 1)
            for step in range(2, n_row):
                if w == 0:
                    @above(step)
                    def _():
                        pl.semaphore_wait(higher, 1)

                        @below(1)
                        def _():
                            tell_below()

                relay(w, step)

    with scope("D_rhs"):
        loads[4].wait()
        loads[5].wait()
        chosen = lax.rem(layer + side, 2)
    with scope("E_lowerw"):
        lower_pair.wait_recv()
    def x_turned(w, which):
        strips = x_all[w, pl.ds(which * n_row, n_row)]
        pieces = [
            jnp.concatenate([strips[r][:, g * strip:(g + 1) * strip] for g in range(pack)], axis=0)
            for r in range(n_row)
        ]
        return jnp.concatenate(pieces, axis=1)

    def part_copy(j, dh, dp, dq):
        rows = pl.ds(pl.multiple_of(j * span + lax.rem(quota + dq, shares) * share, share), share)
        return pltpu.make_async_remote_copy(
            src_ref=part.at[dh * 2 + dp, rows], dst_ref=part_in.at[j, number(*back(dh, dp, dq))],
            send_sem=part_send.at[0], recv_sem=part_recv.at[j],
            device_id=peer(dh, dp, dq), device_id_type=MESH,
        )

    def product(x_own, x_else, dh, dp):
        b = lax.rem(half + dh, halves) * 2 + lax.rem(layer + dp, 2)
        across = pl.ds(pl.multiple_of(b * block, block), block)
        return dot(x_own, lower_all[0, :, across]) + dot(x_else, lower_all[1, :, across])

    near_count = sum(step[0] == 0 for step in straights)
    x_t, later = [], ()
    for w in range(waves):
        with scope(f"F{w}_xw"):
            for r in range(n_row):
                @pl.when(row == r)
                def _():
                    await_bytes(x_all.at[w, pl.ds(0, 2 * n_row - 1 - (2 if r else 0))], x_recv.at[2 * w + 1])
        with scope(f"G{w}_turn"):
            x_t.append((x_turned(w, side), x_turned(w, other)))
        within = range(w * (chunks // waves), (w + 1) * (chunks // waves))
        for j in later:
            for step in group:
                if step[:2] != (0, 0):
                    part_copy(j, *step).start()
        later = within[1:]
        for dh in reversed(range(halves)):
            for dp in reversed(range(2)):
                if (dh, dp) == (0, 0):
                    continue
                with scope(f"H{w}_mm{dh}{dp}"):
                    part[dh * 2 + dp, w * batch:(w + 1) * batch] = product(*x_t[w], dh, dp).astype(jnp.bfloat16)
                    if w == 0 and (dh, dp) == group[0][:2]:
                        pl.semaphore_wait(near, near_count)
                    for step in group:
                        if step[:2] == (dh, dp):
                            part_copy(within[0], *step).start()
    for j in later:
        for step in group:
            if step[:2] != (0, 0):
                part_copy(j, *step).start()
    rhs_pair.start()
    inv_pair.start()
    upper_pair.start()
    with scope("H_own"):
        held[...] = product(*(jnp.concatenate(x, axis=0) for x in zip(*x_t)), 0, 0)
        if shares > 1:
            part[0] = held[...].astype(jnp.bfloat16)
            for j in range(chunks):
                for step in group:
                    if step[:2] == (0, 0):
                        part_copy(j, *step).start()

    own_block = half * 2 + parity

    def anc_copy(j, dh, dp, dq):
        place = anc_t.at[j, own_block, pl.ds(pl.multiple_of(quota * share, share), share)]
        return pltpu.make_async_remote_copy(
            src_ref=place, dst_ref=place,
            send_sem=anc_send.at[0], recv_sem=anc_recv.at[j],
            device_id=peer(dh, dp, dq), device_id_type=MESH,
        )

    with scope("H_rhs"):
        rhs_pair.wait_recv()
        inv_pair.wait_recv()
        rhs_t[...] = rhs_all[chosen].astype(jnp.float32).T
    inverse = inv_all[chosen]
    for j in range(chunks):
        with scope(f"I{j}_partw"):
            await_bytes(part_in.at[j], part_recv.at[j])
        with scope(f"J{j}_solve"):
            rows = pl.ds(pl.multiple_of(j * span + quota * share, share), share)
            remain = rhs_t[rows, :] - held[rows, :]
            for index in range(len(group)):
                remain = remain - part_in[j, index].astype(jnp.float32)
            high = remain.astype(jnp.bfloat16)
            rest = remain - high.astype(jnp.float32)
            middle = rest.astype(jnp.bfloat16)
            low = (rest - middle.astype(jnp.float32)).astype(jnp.bfloat16)
            terms = dot_last(jnp.concatenate([high, middle, low], axis=0), inverse)
            solved = terms[:share] + (terms[share:2 * share] + terms[2 * share:])
            anc_t[j, own_block, pl.ds(pl.multiple_of(quota * share, share), share)] = solved.astype(jnp.bfloat16)
            for step in group:
                anc_copy(j, *step).start()
    with scope("K_upperw"):
        upper_pair.wait_recv()

    def fold_copy(j, dr, which):
        to_row = lax.rem(row + dr, n_row)
        return pltpu.make_async_remote_copy(
            src_ref=fold.at[j, which, to_row], dst_ref=fold_in.at[j, which * n_row + dr],
            send_sem=fold_send.at[0], recv_sem=fold_recv.at[j],
            device_id=(layer, to_row, partner if which else col), device_id_type=MESH,
        )

    anc_pair = [pair_copy(4, anc_t.at[j, partner], anc_other.at[j]) for j in range(chunks)]
    blocks_down = upper_all.shape[1] // block
    strips = block // strip
    for j in range(chunks):
        with scope(f"L{j}_ancw"):
            await_bytes(part_in.at[j], anc_recv.at[j])
        with scope(f"M{j}_mm"):
            solved = jnp.concatenate([anc_t[j, b] for b in range(n_col)], axis=1)
            totals = [
                [
                    dot_last(upper_all[which, i * block:(i + 1) * block, :], solved).astype(jnp.bfloat16)
                    for i in range(blocks_down)
                ]
                for which in range(2)
            ]
        with scope(f"N{j}_pack"):
            for which in range(2):
                for i in range(blocks_down):
                    for s in range(strips):
                        piece = totals[which][i][s * strip:(s + 1) * strip].reshape(chunks, strip // chunks, span)
                        fold[j, which, i * strips + s] = jnp.concatenate([piece[g] for g in range(chunks)], axis=1)
            for dr in reversed(range(n_row)):
                for which in (0, 1) if dr else (1,):
                    fold_copy(j, dr, which).start()
            anc_pair[j].start()

    with scope("O_ancout"):
        await_bytes(anc_other, pair_recv.at[4])
        anc_out[:, columns(side)] = jnp.concatenate([anc_t[j, col] for j in range(chunks)], axis=0).T
        anc_out[:, columns(other)] = jnp.concatenate([anc_other[j] for j in range(chunks)], axis=0).T
    sums = []
    for j in range(chunks):
        with scope(f"P{j}_foldw"):
            await_bytes(fold_in.at[j, pl.ds(1, 2 * n_row - 1)], fold_recv.at[j])
        own = fold[j, 0, row].astype(jnp.float32)
        for dr in range(1, n_row):
            own = own + fold_in[j, dr].astype(jnp.float32)
        others = fold_in[j, n_row].astype(jnp.float32)
        for dr in range(1, n_row):
            others = others + fold_in[j, n_row + dr].astype(jnp.float32)
        sums.append((own, others))
    with scope("Q_out"):
        for which, target in enumerate((side, other)):
            correct = jnp.concatenate(
                [
                    jnp.concatenate([sums[j][which][:, g * span:(g + 1) * span] for j in range(chunks)], axis=1)
                    for g in range(chunks)
                ],
                axis=0,
            )
            new_leaves[0, :, columns(target)] = (leaf_v[:, columns(target)].astype(jnp.float32) - correct).astype(jnp.bfloat16)

    with scope("R_drain"):
        for copy in (lower_pair, upper_pair, rhs_pair, inv_pair):
            copy.wait_send()
        await_bytes(anc_other, pair_send.at[4])
        for r in range(n_row):
            @pl.when(row == r)
            def _():
                await_bytes(x_all.at[:, pl.ds(0, 2 * r + 1 + (2 if r < n_row - 1 else 0))], x_send.at[0])
                if 0 < r < n_row - 1:
                    await_bytes(x_all.at[:, pl.ds(0, 2 * (n_row - 1 - r))], x_send.at[1])

        await_bytes(part_in, part_send.at[0])
        await_bytes(part_in, anc_send.at[0])
        await_bytes(fold_in.at[:, pl.ds(1, 2 * n_row - 1)], fold_send.at[0])


def finish(leaves, anc, leaves_out, anc_out, sem):
    copies = [
        pltpu.make_async_copy(anc, anc_out, sem.at[0]),
        pltpu.make_async_copy(leaves, leaves_out, sem.at[1]),
    ]
    for copy in copies:
        copy.start()
    for copy in copies:
        copy.wait()


def shards(n_layer, n_row, n_col, leaf_sol, lower_blocks, lower_mask, upper_blocks, upper_mask, anc_rhs, diag_inv):
    block = diag_inv.shape[1]
    width = leaf_sol.shape[2]
    strip = leaf_sol.shape[1]
    chunks, waves = 2, 2
    wide = width // 2
    span = wide // chunks
    share = span // (n_layer // 2)
    peers = n_layer * n_col // 2 - 1
    bf16, f32 = jnp.bfloat16, jnp.float32
    anywhere = pl.BlockSpec(memory_space=pltpu.HBM)
    lower_marks = lower_mask.T
    vmem = pl.BlockSpec(memory_space=pltpu.VMEM)
    dma = lambda *sizes: [pltpu.SemaphoreType.DMA((size,)) for size in sizes]
    out_shape = (
        jax.ShapeDtypeStruct(leaf_sol.shape, bf16),
        jax.ShapeDtypeStruct(anc_rhs.shape, bf16),
    )
    results = pl.pallas_call(
        functools.partial(kernel, n_layer, n_row, n_col, chunks, waves),
        out_shape=(pltpu.VMEM(leaf_sol.shape, bf16), pltpu.VMEM(anc_rhs.shape, bf16)),
        in_specs=[anywhere] * 7,
        out_specs=(vmem, vmem),
        scratch_shapes=[
            pltpu.SMEM(lower_marks.shape, jnp.int32),
            pltpu.SMEM(upper_mask.shape, jnp.int32),
            pltpu.VMEM((strip, width), bf16),
            pltpu.VMEM(lower_blocks.shape, bf16),
            pltpu.VMEM((2, *lower_blocks.shape[::-1]), bf16),
            pltpu.VMEM((2, *upper_blocks.shape), bf16),
            pltpu.VMEM((2, block, wide), bf16),
            pltpu.VMEM((2, block, block), bf16),
            pltpu.VMEM((2, waves, strip // waves, wide), bf16),
            pltpu.VMEM((waves, 2 * n_row, strip // waves, wide), bf16),
            pltpu.VMEM((wide, block), f32),
            pltpu.VMEM((wide, block), f32),
            pltpu.VMEM((n_col, wide, block), bf16),
            pltpu.VMEM((chunks, peers, share, block), bf16),
            pltpu.VMEM((chunks, n_col, span, block), bf16),
            pltpu.VMEM((chunks, span, block), bf16),
            pltpu.VMEM((chunks, 2, n_row, strip // chunks, wide), bf16),
            pltpu.VMEM((chunks, 2 * n_row, strip // chunks, wide), bf16),
            *dma(7, 5, 5, 2, 2 * waves, 1, chunks, 1, chunks, 1, chunks),
            pltpu.SemaphoreType.REGULAR,
            pltpu.SemaphoreType.REGULAR,
        ],
        compiler_params=pltpu.CompilerParams(
            collective_id=0, has_side_effects=True,
        ),
    )(leaf_sol, lower_blocks, lower_marks, upper_blocks, upper_mask, anc_rhs, diag_inv)
    anyplace = pl.BlockSpec(memory_space=pl.ANY)
    return pl.pallas_call(
        finish,
        out_shape=out_shape,
        in_specs=[anyplace] * 2,
        out_specs=(anyplace, anyplace),
        scratch_shapes=dma(2),
        compiler_params=pltpu.CompilerParams(vmem_limit_bytes=1024 * 1024),
    )(*results)


def solution(mesh):
    in_specs = (
        P(("layer", "col"), "row", None),
        P(("layer", "row"), "col"),
        P(("layer", "row"), "col"),
        P(("layer", "col"), "row"),
        P(("layer", "col"), "row"),
        P(("row", "col"), None),
        P(("row", "col"), None),
    )
    out_specs = (P(("layer", "col"), "row", None), P(("row", "col"), None))
    body = functools.partial(shards, mesh.shape["layer"], mesh.shape["row"], mesh.shape["col"])
    return jax.shard_map(body, mesh=mesh, in_specs=in_specs, out_specs=out_specs, check_vma=False)
```
